32 devices in a mesh: groups: 2 (over y), space: 8 (over z, x), batch: 2 (over core).
Axes of the slice: x: 2, y: 2, z: 4, core: 2. Of those that a mesh axis runs over, the one named last changes fastest.
Arguments:
- inputs: bfloat16 [4, 8, 8, 8, 8, 1024], P(('groups', 'batch'), 'space'), parts along dimension 0, may hold values from -6 to 6
- cotangent: bfloat16 [4, 8, 8, 8, 8, 1024], P(('groups', 'batch'), 'space'), parts along dimension 0, may hold values from -6 to 6
- offsets: int32 [4], P(('groups', 'batch')), parts along dimension 0, may hold values from 1 to 7
- w_qkv: bfloat16 [1024, 3072], P('batch'), may hold values from -0.375 to 0.375
- w_out: bfloat16 [1024, 1024], P('batch'), may hold values from -0.1875 to 0.1875
- gain: float32 [1024], replicated, may hold values from 0.5 to 2, as said below
Outputs:
- update: bfloat16 [4, 8, 8, 8, 8, 1024], P(('groups', 'batch'), 'space'), parts along dimension 0
- grad: bfloat16 [4, 8, 8, 8, 8, 1024], P(('groups', 'batch'), 'space'), parts along dimension 0
The draws below stay inside these ranges and needn't reach their ends.
There are 2 independent parts, one for each index of `groups`. The reference program is written for one: setup_inputs(seed, part) draws one part's arguments, and reference() takes and returns one part's arrays. A program takes and returns all parts, laid end to end along the dimension named above; an argument that names none is the same for every part. Nothing has to cross between parts.
Inputs may be any that keep to these rules, and one draw needn't show every extreme that they name: `gain`: positive gains.
All inputs are finite; a program needn't handle non-finite values.
Results may differ from the reference program's by a relative error of at most 0.005.
The reference program's roundings to bfloat16 on the way count: a program that leaves them out, or rounds other values in their place, can miss the bound.
Values may be sent and summed in bfloat16 or wider, within the bound.
A program may use at most 128 MiB of HBM per device.

```python
import jax
import jax.numpy as jnp
from jax import lax

D = 1024
WIN = 8
YTILES = 4
GZ = 8
HEAD_DIM = 64
CANDS = 2
XTILES = 2
N_SPACE = 8


def draw_gain(key, part):
    return 1.0 + 0.3 * jax.random.uniform(key, (D,), jnp.float32, -1.0, 1.0)


def level_of(own_key, extent, pieces, least, high):
    factor_of, own = 1.0, jax.random.fold_in(own_key, 6)
    for position, parts in pieces:
        heights = jnp.exp(jax.random.uniform(jax.random.fold_in(own, position), (parts,), jnp.float32, least / len(pieces), high / len(pieces)))
        factor_of = factor_of * jnp.repeat(heights, extent[position] // parts).reshape([-1 if axis == position else 1 for axis in range(len(extent))])
    return factor_of


def centred(stream_key, shape, scale, bound, shards=(), dtype=jnp.bfloat16):
    level = level_of(stream_key, shape, shards, -0.22, 0.18) if shards else 1.0
    result = jax.random.normal(stream_key, shape, jnp.float32) * scale * level
    return jnp.minimum(jnp.maximum(result, -bound), bound).astype(dtype)


def setup_inputs(seed: int = 0, part: int = 0) -> dict:
    key_list = jax.random.split(jax.random.key(seed), 7)
    part_keys = jax.random.split(jax.random.fold_in(key_list[6], part), 7)
    inputs = centred(part_keys[0], (CANDS, N_SPACE, WIN, WIN, GZ, D), 1.0, 6.0, ((0, 2), (1, 8)))
    cotangent = centred(part_keys[1], (CANDS, N_SPACE, WIN, WIN, GZ, D), 1.0, 6.0, ((0, 2), (1, 8)))
    offsets = jax.random.randint(part_keys[2], (CANDS,), 1, WIN).astype(jnp.int32)
    w_qkv = centred(key_list[3], (D, 3 * D), (D // 4) ** -0.5, 0.375, ((0, 2),))
    w_out = centred(key_list[4], (D, D), D ** -0.5, 0.1875, ((0, 2),))
    gain = draw_gain(jax.random.fold_in(key_list[6], 71), part)
    return dict(inputs=inputs, cotangent=cotangent, offsets=offsets, w_qkv=w_qkv, w_out=w_out, gain=gain)


EPS = 1e-05
GROUP_HEADS = 4

def to_windows(grid_field):
    extent_x, extent_y, extent_z, channels = grid_field.shape
    window_side = WIN
    blocks = grid_field.reshape(extent_x // window_side, window_side, extent_y // window_side, window_side, extent_z // window_side, window_side, channels)
    blocks = blocks.transpose(0, 2, 4, 1, 3, 5, 6)
    return blocks.reshape(-1, window_side * window_side * window_side, channels)

def from_windows(window_stack, extent_x, extent_y, extent_z):
    window_side = WIN
    channels = window_stack.shape[-1]
    blocks = window_stack.reshape(extent_x // window_side, extent_y // window_side, extent_z // window_side, window_side, window_side, window_side, channels)
    blocks = blocks.transpose(0, 3, 1, 4, 2, 5, 6)
    return blocks.reshape(extent_x, extent_y, extent_z, channels)

def tiles_to_grid(tiled):
    channels = tiled.shape[-1]
    blocks = tiled.reshape(XTILES, YTILES, WIN, WIN, tiled.shape[3], channels)
    return blocks.transpose(0, 2, 1, 3, 4, 5).reshape(XTILES * WIN, YTILES * WIN, tiled.shape[3], channels)

def grid_to_tiles(grid_field):
    extent_z, channels = (grid_field.shape[2], grid_field.shape[3])
    blocks = grid_field.reshape(XTILES, WIN, YTILES, WIN, extent_z, channels)
    return blocks.transpose(0, 2, 1, 3, 4, 5).reshape(XTILES * YTILES, WIN, WIN, extent_z, channels)

def split_heads(matrix):
    row_count = matrix.shape[0]
    return matrix.reshape(row_count, -1, GROUP_HEADS, HEAD_DIM).transpose(1, 0, 2, 3)

def join_heads(grouped):
    return grouped.transpose(1, 0, 2, 3).reshape(grouped.shape[1], -1)

def group_scores(query, keys):
    return jnp.einsum('qhd,khd->hqk', query.astype(jnp.float32), keys.astype(jnp.float32)) * HEAD_DIM ** (-0.5)

def probabilities(scores):
    peak = lax.optimization_barrier(jnp.max(scores, axis=-1, keepdims=True))
    raised = jnp.exp(scores - peak)
    return raised / lax.optimization_barrier(jnp.sum(raised, axis=-1, keepdims=True))

def attend_group(operands):
    query, keys, values = operands
    soft_low = probabilities(group_scores(query, keys)).astype(jnp.bfloat16)
    return jnp.einsum('hqk,khd->qhd', soft_low.astype(jnp.float32), values.astype(jnp.float32)).astype(jnp.bfloat16)

def reverse_group(operands):
    query, keys, values, upstream = operands
    soft = probabilities(group_scores(query, keys))
    grad_weights = jnp.einsum('qhd,khd->hqk', upstream.astype(jnp.float32), values.astype(jnp.float32))
    grad_scores = (soft * (grad_weights - lax.optimization_barrier(jnp.sum(grad_weights * soft, axis=-1, keepdims=True))) * HEAD_DIM ** (-0.5)).astype(jnp.bfloat16)
    grad_float = grad_scores.astype(jnp.float32)
    grad_query = jnp.einsum('hqk,khd->qhd', grad_float, keys.astype(jnp.float32)).astype(jnp.bfloat16)
    grad_keys = jnp.einsum('hqk,qhd->khd', grad_float, query.astype(jnp.float32)).astype(jnp.bfloat16)
    soft_low = soft.astype(jnp.bfloat16).astype(jnp.float32)
    grad_values = jnp.einsum('hqk,qhd->khd', soft_low, upstream.astype(jnp.float32)).astype(jnp.bfloat16)
    return (grad_query, grad_keys, grad_values)

def window_block(tokens, cot_tokens, w_qkv, w_out, gain):
    channels = tokens.shape[1]
    values32 = tokens.astype(jnp.float32)
    center = values32 - lax.optimization_barrier(jnp.mean(values32, axis=-1, keepdims=True))
    inverse = lax.rsqrt(lax.optimization_barrier(jnp.mean(center * center, axis=-1, keepdims=True)) + EPS)
    normed = center * inverse
    scaled = (normed * gain).astype(jnp.bfloat16)
    projected = jnp.dot(scaled, w_qkv, preferred_element_type=jnp.float32)
    query = projected[:, :channels].astype(jnp.bfloat16)
    keys = projected[:, channels:2 * channels].astype(jnp.bfloat16)
    values = projected[:, 2 * channels:].astype(jnp.bfloat16)
    grouped = (split_heads(query), split_heads(keys), split_heads(values))
    attended = join_heads(lax.map(attend_group, grouped))
    frame_update = jnp.dot(attended, w_out, preferred_element_type=jnp.float32).astype(jnp.bfloat16)
    upstream = jnp.dot(cot_tokens, w_out.T, preferred_element_type=jnp.float32).astype(jnp.bfloat16)
    grad_query, grad_keys, grad_values = lax.map(reverse_group, grouped + (split_heads(upstream),))
    grad_qkv = jnp.concatenate([join_heads(grad_query), join_heads(grad_keys), join_heads(grad_values)], axis=1)
    grad_normed = jnp.dot(grad_qkv, w_qkv.T, preferred_element_type=jnp.float32) * gain
    mean_grad = lax.optimization_barrier(jnp.mean(grad_normed, axis=-1, keepdims=True))
    mean_mixed = lax.optimization_barrier(jnp.mean(grad_normed * normed, axis=-1, keepdims=True))
    frame_grad = (inverse * (grad_normed - mean_grad - normed * mean_mixed)).astype(jnp.bfloat16)
    return (frame_update, frame_grad)

def reference(inputs, cotangent, offsets, w_qkv, w_out, gain):

    def candidate(operands):
        tiled_in, tiled_cot, start = operands
        grid_in = tiles_to_grid(tiled_in)
        grid_cot = tiles_to_grid(tiled_cot)
        extent_x, extent_y, extent_z = (grid_in.shape[0], grid_in.shape[1], grid_in.shape[2])
        rolled_in = to_windows(jnp.roll(grid_in, -start, axis=0))
        rolled_cot = to_windows(jnp.roll(grid_cot, -start, axis=0))

        def one_window(pair):
            return window_block(pair[0], pair[1], w_qkv, w_out, gain)
        updates, grads = lax.map(one_window, (rolled_in, rolled_cot))
        update_grid = jnp.roll(from_windows(updates, extent_x, extent_y, extent_z), start, axis=0)
        grad_grid = jnp.roll(from_windows(grads, extent_x, extent_y, extent_z), start, axis=0)
        return (grid_to_tiles(update_grid), grid_to_tiles(grad_grid))
    update, grad = lax.map(candidate, (inputs, cotangent, offsets.astype(jnp.int32)))
    return (update, grad)
```

```python
import jax
import jax.numpy as jnp
from jax import lax
from jax.experimental import pallas as pl
from jax.experimental.pallas import tpu as pltpu
from jax.sharding import PartitionSpec as P

YTILES = 4
HEAD_DIM = 64
EPS = 1e-05
PAIR = 2 * HEAD_DIM
SCALE = HEAD_DIM ** (-0.5)


def passed_along(x, by):
    size = lax.axis_size("space")
    return lax.ppermute(x, "space", [(i, (i + by) % size) for i in range(size)])


def nt(a, b):
    return lax.dot_general(a, b, (((1,), (1,)), ((), ())), preferred_element_type=jnp.float32)


def nn(a, b):
    return lax.dot_general(a, b, (((1,), (0,)), ((), ())), preferred_element_type=jnp.float32)


def only_head(x, head):
    lane = lax.broadcasted_iota(jnp.int32, x.shape, 1)
    keep = lane < HEAD_DIM if head == 0 else lane >= HEAD_DIM
    return jnp.where(keep, x, jnp.zeros_like(x))


def by_head(first, second):
    lane = lax.broadcasted_iota(jnp.int32, first.shape, 1)
    return jnp.where(lane < HEAD_DIM, first, second)


def attend_kernel(q_ref, k_ref, v_ref, o_ref, stats_ref):
    q, k = q_ref[...], k_ref[...]
    v_t = v_ref[...].T
    outs = []
    for head in range(2):
        scores = nt(k, only_head(q, head)) * SCALE
        peak = jnp.max(scores, axis=0, keepdims=True)
        raised = jnp.exp(scores - peak)
        inv = 1.0 / jnp.sum(raised, axis=0, keepdims=True)
        stats_ref[0, 2 * head : 2 * head + 1, :] = peak
        stats_ref[0, 2 * head + 1 : 2 * head + 2, :] = inv
        probs = (raised * inv).astype(jnp.bfloat16)
        outs.append(nn(v_t[HEAD_DIM * head : HEAD_DIM * (head + 1)], probs))
    o_ref[...] = jnp.concatenate(outs, axis=0).T.astype(jnp.bfloat16)


def reverse_kernel(q_ref, k_ref, v_ref, up_ref, stats_ref, dq_ref, dk_ref, dv_ref):
    q, k, v, up = q_ref[...], k_ref[...], v_ref[...], up_ref[...]
    k_t = k.T
    dqs, dks, dvs = [], [], []
    for head in range(2):
        scores = nt(k, only_head(q, head)) * SCALE
        peak = stats_ref[0, 2 * head : 2 * head + 1, :]
        inv = stats_ref[0, 2 * head + 1 : 2 * head + 2, :]
        probs = jnp.exp(scores - peak) * inv
        grad_probs = nt(v, only_head(up, head))
        delta = jnp.sum(grad_probs * probs, axis=0, keepdims=True)
        grad_scores = (probs * (grad_probs - delta) * SCALE).astype(jnp.bfloat16)
        dqs.append(nn(k_t[HEAD_DIM * head : HEAD_DIM * (head + 1)], grad_scores))
        dks.append(nn(grad_scores, q))
        dvs.append(nn(probs.astype(jnp.bfloat16), up))
    dq_ref[...] = jnp.concatenate(dqs, axis=0).T.astype(jnp.bfloat16)
    dk_ref[...] = by_head(*dks).astype(jnp.bfloat16)
    dv_ref[...] = by_head(*dvs).astype(jnp.bfloat16)


def attend(qkv):
    tokens, width = qkv.shape
    channels = width // 3
    pairs = channels // PAIR

    def cols(which):
        return pl.BlockSpec((tokens, PAIR), lambda i: (0, which * pairs + i))

    return pl.pallas_call(
        attend_kernel,
        grid=(pairs,),
        in_specs=[cols(0), cols(1), cols(2)],
        out_specs=[cols(0), pl.BlockSpec((1, 4, tokens), lambda i: (i, 0, 0))],
        out_shape=[
            jax.ShapeDtypeStruct((tokens, channels), jnp.bfloat16),
            jax.ShapeDtypeStruct((pairs, 4, tokens), jnp.float32),
        ],
        compiler_params=pltpu.CompilerParams(vmem_limit_bytes=40 << 20),
        cost_estimate=pl.CostEstimate(
            flops=8 * tokens * tokens * channels,
            transcendentals=tokens * tokens * channels // HEAD_DIM,
            bytes_accessed=8 * tokens * channels,
        ),
        name="attend",
    )(qkv, qkv, qkv)


def reverse(qkv, up, stats):
    tokens, width = qkv.shape
    channels = width // 3
    pairs = channels // PAIR

    def cols(which):
        return pl.BlockSpec((tokens, PAIR), lambda i: (0, which * pairs + i))

    return pl.pallas_call(
        reverse_kernel,
        grid=(pairs,),
        in_specs=[cols(0), cols(1), cols(2), cols(0), pl.BlockSpec((1, 4, tokens), lambda i: (i, 0, 0))],
        out_specs=[cols(0), cols(0), cols(0)],
        out_shape=[jax.ShapeDtypeStruct((tokens, channels), jnp.bfloat16)] * 3,
        compiler_params=pltpu.CompilerParams(vmem_limit_bytes=40 << 20),
        cost_estimate=pl.CostEstimate(
            flops=20 * tokens * tokens * channels,
            transcendentals=tokens * tokens * channels // HEAD_DIM,
            bytes_accessed=14 * tokens * channels,
        ),
        name="reverse",
    )(qkv, qkv, qkv, up, stats)


def normalise(x):
    values32 = x.astype(jnp.float32)
    center = values32 - jnp.mean(values32, axis=-1, keepdims=True)
    inverse = lax.rsqrt(jnp.mean(center * center, axis=-1, keepdims=True) + EPS)
    return center * inverse, inverse


def shards(inputs, cotangent, offsets, w_qkv, w_out, gain):
    tiled_shape = inputs.shape
    slab, channels = tiled_shape[2], tiled_shape[-1]
    inputs = inputs.reshape(-1, channels)
    cotangent = cotangent.reshape(-1, channels)
    tokens = inputs.shape[0]
    half, plane = tokens // 2, tokens // slab
    start = offsets[0]
    upper = start > slab // 2
    two = lax.axis_size("space") == 2 * YTILES
    plane_of = lax.broadcasted_iota(jnp.int32, (half, 1), 0) // plane
    foreign = jnp.where(upper, plane_of + slab // 2 >= start, plane_of < start)

    def edge(x):
        return lax.dynamic_slice_in_dim(x, jnp.where(upper, half, 0), half, 0)

    def core(x):
        return lax.dynamic_slice_in_dim(x, jnp.where(upper, 0, half), half, 0)

    def fetch(x):
        if two:
            return passed_along(edge(x), YTILES)
        return jnp.where(upper, passed_along(x[half:], YTILES), passed_along(x[:half], -YTILES))

    def give_back(x):
        if two:
            return passed_along(x, YTILES)
        return jnp.where(upper, passed_along(x, -YTILES), passed_along(x, YTILES))

    def place(edge_mine, edge_back, core_mine):
        edge_out = jnp.where(foreign, edge_back, edge_mine)
        low = jnp.where(upper, core_mine, edge_out)
        high = jnp.where(upper, edge_out, core_mine)
        return jnp.concatenate([low, high], axis=0).reshape(tiled_shape)

    in_far = fetch(inputs)
    cot_far = fetch(cotangent)
    all_qkv = lax.all_gather(w_qkv, "batch", axis=0, tiled=True)
    all_out = lax.all_gather(w_out, "batch", axis=0, tiled=True)

    def project(x):
        normed, inverse = normalise(x)
        scaled = (normed * gain).astype(jnp.bfloat16)
        return nn(scaled, all_qkv).astype(jnp.bfloat16)

    in_core, cot_core = core(inputs), core(cotangent)
    qkv_core = project(in_core)
    up_core = nt(cot_core, all_out).astype(jnp.bfloat16)
    in_edge = jnp.where(foreign, in_far, edge(inputs))
    qkv_edge = project(in_edge)
    qkv = jnp.concatenate([qkv_edge, qkv_core], axis=0)
    attended, stats = attend(qkv)
    up_edge_rows = nn(attended[:half], all_out).astype(jnp.bfloat16)
    update_back = give_back(up_edge_rows)
    update_core = nn(attended[half:], all_out).astype(jnp.bfloat16)

    cot_edge = jnp.where(foreign, cot_far, edge(cotangent))
    up = jnp.concatenate([nt(cot_edge, all_out).astype(jnp.bfloat16), up_core], axis=0)
    grads = reverse(qkv, up, stats)

    def backward(rows, x):
        total = 0.0
        for index, piece in enumerate(grads):
            total = total + nt(piece[rows], all_qkv[:, index * channels : (index + 1) * channels])
        grad_normed = total * gain
        normed, inverse = normalise(x)
        mean_grad = jnp.mean(grad_normed, axis=-1, keepdims=True)
        mean_mixed = jnp.mean(grad_normed * normed, axis=-1, keepdims=True)
        return (inverse * (grad_normed - mean_grad - normed * mean_mixed)).astype(jnp.bfloat16)

    grad_edge = backward(slice(0, half), in_edge)
    grad_back = give_back(grad_edge)
    grad_core = backward(slice(half, tokens), in_core)
    update = place(up_edge_rows, update_back, update_core)
    grad = place(grad_edge, grad_back, grad_core)
    return update, grad


def solution(mesh):
    tiles = P(("groups", "batch"), "space", None, None, None, None)
    in_specs = (tiles, tiles, P(("groups", "batch")), P("batch", None), P("batch", None), P())
    return jax.shard_map(shards, mesh=mesh, in_specs=in_specs, out_specs=(tiles, tiles), check_vma=False)
```

```python
import jax
import jax.numpy as jnp
from jax import lax
from jax.experimental import pallas as pl
from jax.experimental.pallas import tpu as pltpu
from jax.sharding import PartitionSpec as P

YTILES = 4
HEAD_DIM = 64
EPS = 1e-05
PAIR = 2 * HEAD_DIM
SCALE = HEAD_DIM ** (-0.5)


def passed_along(x, by):
    size = lax.axis_size("space")
    return lax.ppermute(x, "space", [(i, (i + by) % size) for i in range(size)])


def nt(a, b):
    return lax.dot_general(a, b, (((1,), (1,)), ((), ())), preferred_element_type=jnp.float32)


def nn(a, b):
    return lax.dot_general(a, b, (((1,), (0,)), ((), ())), preferred_element_type=jnp.float32)


def only_head(x, head):
    lane = lax.broadcasted_iota(jnp.int32, x.shape, 1)
    keep = lane < HEAD_DIM if head == 0 else lane >= HEAD_DIM
    return jnp.where(keep, x, jnp.zeros_like(x))


def by_head(first, second):
    lane = lax.broadcasted_iota(jnp.int32, first.shape, 1)
    return jnp.where(lane < HEAD_DIM, first, second)


def attend_kernel(q_ref, k_ref, v_ref, o_ref, stats_ref):
    q, k = q_ref[...], k_ref[...]
    v_t = v_ref[...].T
    outs = []
    for head in range(2):
        scores = nt(k, only_head(q, head)) * SCALE
        peak = jnp.max(scores, axis=0, keepdims=True)
        raised = jnp.exp(scores - peak)
        inv = 1.0 / jnp.sum(raised, axis=0, keepdims=True)
        stats_ref[0, 2 * head : 2 * head + 1, :] = peak
        stats_ref[0, 2 * head + 1 : 2 * head + 2, :] = inv
        probs = (raised * inv).astype(jnp.bfloat16)
        outs.append(nn(v_t[HEAD_DIM * head : HEAD_DIM * (head + 1)], probs))
    o_ref[...] = jnp.concatenate(outs, axis=0).T.astype(jnp.bfloat16)


def reverse_kernel(q_ref, k_ref, v_ref, up_ref, stats_ref, dq_ref, dk_ref, dv_ref):
    q, k, v, up = q_ref[...], k_ref[...], v_ref[...], up_ref[...]
    k_t = k.T
    dqs, dks, dvs = [], [], []
    for head in range(2):
        scores = nt(k, only_head(q, head)) * SCALE
        peak = stats_ref[0, 2 * head : 2 * head + 1, :]
        inv = stats_ref[0, 2 * head + 1 : 2 * head + 2, :]
        probs = jnp.exp(scores - peak) * inv
        grad_probs = nt(v, only_head(up, head))
        delta = jnp.sum(grad_probs * probs, axis=0, keepdims=True)
        grad_scores = (probs * (grad_probs - delta) * SCALE).astype(jnp.bfloat16)
        dqs.append(nn(k_t[HEAD_DIM * head : HEAD_DIM * (head + 1)], grad_scores))
        dks.append(nn(grad_scores, q))
        dvs.append(nn(probs.astype(jnp.bfloat16), up))
    dq_ref[...] = jnp.concatenate(dqs, axis=0).T.astype(jnp.bfloat16)
    dk_ref[...] = by_head(*dks).astype(jnp.bfloat16)
    dv_ref[...] = by_head(*dvs).astype(jnp.bfloat16)


def attend(qkv):
    tokens, width = qkv.shape
    channels = width // 3
    pairs = channels // PAIR

    def cols(which):
        return pl.BlockSpec((tokens, PAIR), lambda i: (0, which * pairs + i))

    return pl.pallas_call(
        attend_kernel,
        grid=(pairs,),
        in_specs=[cols(0), cols(1), cols(2)],
        out_specs=[cols(0), pl.BlockSpec((1, 4, tokens), lambda i: (i, 0, 0))],
        out_shape=[
            jax.ShapeDtypeStruct((tokens, channels), jnp.bfloat16),
            jax.ShapeDtypeStruct((pairs, 4, tokens), jnp.float32),
        ],
        compiler_params=pltpu.CompilerParams(vmem_limit_bytes=40 << 20),
        cost_estimate=pl.CostEstimate(
            flops=8 * tokens * tokens * channels,
            transcendentals=tokens * tokens * channels // HEAD_DIM,
            bytes_accessed=8 * tokens * channels,
        ),
        name="attend",
    )(qkv, qkv, qkv)


def reverse(qkv, up, stats):
    tokens, width = qkv.shape
    channels = width // 3
    pairs = channels // PAIR

    def cols(which):
        return pl.BlockSpec((tokens, PAIR), lambda i: (0, which * pairs + i))

    return pl.pallas_call(
        reverse_kernel,
        grid=(pairs,),
        in_specs=[cols(0), cols(1), cols(2), cols(0), pl.BlockSpec((1, 4, tokens), lambda i: (i, 0, 0))],
        out_specs=[cols(0), cols(0), cols(0)],
        out_shape=[jax.ShapeDtypeStruct((tokens, channels), jnp.bfloat16)] * 3,
        compiler_params=pltpu.CompilerParams(vmem_limit_bytes=40 << 20),
        cost_estimate=pl.CostEstimate(
            flops=20 * tokens * tokens * channels,
            transcendentals=tokens * tokens * channels // HEAD_DIM,
            bytes_accessed=14 * tokens * channels,
        ),
        name="reverse",
    )(qkv, qkv, qkv, up, stats)


def normalise(x):
    values32 = x.astype(jnp.float32)
    center = values32 - jnp.mean(values32, axis=-1, keepdims=True)
    inverse = lax.rsqrt(jnp.mean(center * center, axis=-1, keepdims=True) + EPS)
    return center * inverse, inverse


def shards(inputs, cotangent, offsets, w_qkv, w_out, gain):
    tiled_shape = inputs.shape
    slab, channels = tiled_shape[2], tiled_shape[-1]
    inputs = inputs.reshape(-1, channels)
    cotangent = cotangent.reshape(-1, channels)
    tokens = inputs.shape[0]
    half, plane = tokens // 2, tokens // slab
    start = offsets[0]
    upper = start > slab // 2
    two = lax.axis_size("space") == 2 * YTILES
    plane_of = lax.broadcasted_iota(jnp.int32, (half, 1), 0) // plane
    foreign = jnp.where(upper, plane_of + slab // 2 >= start, plane_of < start)

    def edge(x):
        return lax.dynamic_slice_in_dim(x, jnp.where(upper, half, 0), half, 0)

    def core(x):
        return lax.dynamic_slice_in_dim(x, jnp.where(upper, 0, half), half, 0)

    def after(x, *earlier):
        return lax.optimization_barrier((x,) + earlier)[0]

    def fetch(x):
        if two:
            return passed_along(edge(x), YTILES)
        return jnp.where(upper, passed_along(x[half:], YTILES), passed_along(x[:half], -YTILES))

    def give_back(x):
        if two:
            return passed_along(x, YTILES)
        return jnp.where(upper, passed_along(x, -YTILES), passed_along(x, YTILES))

    def place(edge_mine, edge_back, core_mine):
        edge_out = jnp.where(foreign, edge_back, edge_mine)
        low = jnp.where(upper, core_mine, edge_out)
        high = jnp.where(upper, edge_out, core_mine)
        return jnp.concatenate([low, high], axis=0).reshape(tiled_shape)

    in_far = fetch(inputs)
    all_qkv = lax.all_gather(w_qkv, "batch", axis=0, tiled=True)
    all_out = lax.all_gather(w_out, "batch", axis=0, tiled=True)

    def project(x):
        normed, inverse = normalise(x)
        scaled = (normed * gain).astype(jnp.bfloat16)
        return nn(scaled, all_qkv).astype(jnp.bfloat16)

    in_core, cot_core = core(inputs), core(cotangent)
    qkv_core = project(in_core)
    up_core = nt(cot_core, all_out).astype(jnp.bfloat16)
    in_far = after(in_far, qkv_core, up_core)
    cot_far = fetch(after(cotangent, in_far))
    in_edge = jnp.where(foreign, in_far, edge(inputs))
    qkv_edge = project(in_edge)
    qkv = jnp.concatenate([qkv_edge, qkv_core], axis=0)
    attended, stats = attend(qkv)
    up_edge_rows = nn(attended[:half], all_out).astype(jnp.bfloat16)
    update_back = give_back(up_edge_rows)
    update_core = nn(attended[half:], all_out).astype(jnp.bfloat16)

    cot_far = after(cot_far, up_edge_rows)
    cot_edge = jnp.where(foreign, cot_far, edge(cotangent))
    up = jnp.concatenate([nt(cot_edge, all_out).astype(jnp.bfloat16), up_core], axis=0)
    grads = reverse(qkv, up, stats)

    def backward(rows, x):
        total = 0.0
        for index, piece in enumerate(grads):
            total = total + nt(piece[rows], all_qkv[:, index * channels : (index + 1) * channels])
        grad_normed = total * gain
        normed, inverse = normalise(x)
        mean_grad = jnp.mean(grad_normed, axis=-1, keepdims=True)
        mean_mixed = jnp.mean(grad_normed * normed, axis=-1, keepdims=True)
        return (inverse * (grad_normed - mean_grad - normed * mean_mixed)).astype(jnp.bfloat16)

    grad_edge = backward(slice(0, half), in_edge)
    grad_back = give_back(grad_edge)
    grad_core = backward(slice(half, tokens), in_core)
    update = place(up_edge_rows, update_back, update_core)
    grad = place(grad_edge, grad_back, grad_core)
    return update, grad


def solution(mesh):
    tiles = P(("groups", "batch"), "space", None, None, None, None)
    in_specs = (tiles, tiles, P(("groups", "batch")), P("batch", None), P("batch", None), P())
    return jax.shard_map(shards, mesh=mesh, in_specs=in_specs, out_specs=(tiles, tiles), check_vma=False)
```

```python
import jax
import jax.numpy as jnp
from jax import lax
from jax.experimental import pallas as pl
from jax.experimental.pallas import tpu as pltpu
from jax.sharding import PartitionSpec as P

YTILES = 4
HEAD_DIM = 64
EPS = 1e-05
PAIR = 2 * HEAD_DIM
SCALE = HEAD_DIM ** (-0.5)


def passed_along(x, by):
    size = lax.axis_size("space")
    return lax.ppermute(x, "space", [(i, (i + by) % size) for i in range(size)])


def nt(a, b):
    return lax.dot_general(a, b, (((1,), (1,)), ((), ())), preferred_element_type=jnp.float32)


def nn(a, b):
    return lax.dot_general(a, b, (((1,), (0,)), ((), ())), preferred_element_type=jnp.float32)


def only_head(x, head):
    lane = lax.broadcasted_iota(jnp.int32, x.shape, 1)
    keep = lane < HEAD_DIM if head == 0 else lane >= HEAD_DIM
    return jnp.where(keep, x, jnp.zeros_like(x))


def by_head(first, second):
    lane = lax.broadcasted_iota(jnp.int32, first.shape, 1)
    return jnp.where(lane < HEAD_DIM, first, second)


def attend_kernel(q_ref, k_ref, v_ref, o_ref, stats_ref):
    q, k = q_ref[...] * SCALE, k_ref[...]
    v_t = v_ref[...].T
    outs = []
    for head in range(2):
        scores = nt(k, only_head(q, head))
        peak = jnp.max(scores, axis=0, keepdims=True)
        raised = jnp.exp(scores - peak)
        inv = 1.0 / jnp.sum(raised, axis=0, keepdims=True)
        stats_ref[0, 2 * head : 2 * head + 1, :] = peak
        stats_ref[0, 2 * head + 1 : 2 * head + 2, :] = inv
        probs = (raised * inv).astype(jnp.bfloat16)
        outs.append(nn(v_t[HEAD_DIM * head : HEAD_DIM * (head + 1)], probs))
    o_ref[...] = jnp.concatenate(outs, axis=0).T.astype(jnp.bfloat16)


def reverse_kernel(q_ref, k_ref, v_ref, up_ref, stats_ref, dq_ref, dk_ref, dv_ref):
    q, k, v, up = q_ref[...] * SCALE, k_ref[...], v_ref[...], up_ref[...]
    k_t = (k * SCALE).T
    dqs, dks, dvs = [], [], []
    for head in range(2):
        scores = nt(k, only_head(q, head))
        peak = stats_ref[0, 2 * head : 2 * head + 1, :]
        inv = stats_ref[0, 2 * head + 1 : 2 * head + 2, :]
        probs = jnp.exp(scores - peak) * inv
        grad_probs = nt(v, only_head(up, head))
        delta = jnp.sum(grad_probs * probs, axis=0, keepdims=True)
        grad_scores = (probs * (grad_probs - delta)).astype(jnp.bfloat16)
        dqs.append(nn(k_t[HEAD_DIM * head : HEAD_DIM * (head + 1)], grad_scores))
        dks.append(nn(grad_scores, q))
        dvs.append(nn(probs.astype(jnp.bfloat16), up))
    dq_ref[...] = jnp.concatenate(dqs, axis=0).T.astype(jnp.bfloat16)
    dk_ref[...] = by_head(*dks).astype(jnp.bfloat16)
    dv_ref[...] = by_head(*dvs).astype(jnp.bfloat16)


def attend(qkv):
    tokens, width = qkv.shape
    channels = width // 3
    pairs = channels // PAIR

    def cols(which):
        return pl.BlockSpec((tokens, PAIR), lambda i: (0, which * pairs + i))

    return pl.pallas_call(
        attend_kernel,
        grid=(pairs,),
        in_specs=[cols(0), cols(1), cols(2)],
        out_specs=[cols(0), pl.BlockSpec((1, 4, tokens), lambda i: (i, 0, 0))],
        out_shape=[
            jax.ShapeDtypeStruct((tokens, channels), jnp.bfloat16),
            jax.ShapeDtypeStruct((pairs, 4, tokens), jnp.float32),
        ],
        compiler_params=pltpu.CompilerParams(vmem_limit_bytes=40 << 20),
        cost_estimate=pl.CostEstimate(
            flops=8 * tokens * tokens * channels,
            transcendentals=tokens * tokens * channels // HEAD_DIM,
            bytes_accessed=8 * tokens * channels,
        ),
        name="attend",
    )(qkv, qkv, qkv)


def reverse(qkv, up, stats):
    tokens, width = qkv.shape
    channels = width // 3
    pairs = channels // PAIR

    def cols(which):
        return pl.BlockSpec((tokens, PAIR), lambda i: (0, which * pairs + i))

    return pl.pallas_call(
        reverse_kernel,
        grid=(pairs,),
        in_specs=[cols(0), cols(1), cols(2), cols(0), pl.BlockSpec((1, 4, tokens), lambda i: (i, 0, 0))],
        out_specs=[cols(0), cols(0), cols(0)],
        out_shape=[jax.ShapeDtypeStruct((tokens, channels), jnp.bfloat16)] * 3,
        compiler_params=pltpu.CompilerParams(vmem_limit_bytes=40 << 20),
        cost_estimate=pl.CostEstimate(
            flops=20 * tokens * tokens * channels,
            transcendentals=tokens * tokens * channels // HEAD_DIM,
            bytes_accessed=14 * tokens * channels,
        ),
        name="reverse",
    )(qkv, qkv, qkv, up, stats)


def normalise(x):
    values32 = x.astype(jnp.float32)
    center = values32 - jnp.mean(values32, axis=-1, keepdims=True)
    inverse = lax.rsqrt(jnp.mean(center * center, axis=-1, keepdims=True) + EPS)
    return center * inverse, inverse


def shards(inputs, cotangent, offsets, w_qkv, w_out, gain):
    tiled_shape = inputs.shape
    slab, channels = tiled_shape[2], tiled_shape[-1]
    inputs = inputs.reshape(-1, channels)
    cotangent = cotangent.reshape(-1, channels)
    tokens = inputs.shape[0]
    half, plane = tokens // 2, tokens // slab
    start = offsets[0]
    upper = start > slab // 2
    two = lax.axis_size("space") == 2 * YTILES
    plane_of = lax.broadcasted_iota(jnp.int32, (half, 1), 0) // plane
    foreign = jnp.where(upper, plane_of + slab // 2 >= start, plane_of < start)

    def edge(x):
        return lax.dynamic_slice_in_dim(x, jnp.where(upper, half, 0), half, 0)

    def core(x):
        return lax.dynamic_slice_in_dim(x, jnp.where(upper, 0, half), half, 0)

    def after(x, *earlier):
        return lax.optimization_barrier((x,) + earlier)[0]

    def fetch(x):
        if two:
            return passed_along(edge(x), YTILES)
        return jnp.where(upper, passed_along(x[half:], YTILES), passed_along(x[:half], -YTILES))

    def give_back(x):
        if two:
            return passed_along(x, YTILES)
        return jnp.where(upper, passed_along(x, -YTILES), passed_along(x, YTILES))

    def place(edge_mine, edge_back, core_mine):
        edge_out = jnp.where(foreign, edge_back, edge_mine)
        low = jnp.where(upper, core_mine, edge_out)
        high = jnp.where(upper, edge_out, core_mine)
        return jnp.concatenate([low, high], axis=0).reshape(tiled_shape)

    first = lax.axis_index("batch") == 0

    def whole(own, other):
        return jnp.concatenate([jnp.where(first, own, other), jnp.where(first, other, own)], axis=0)

    other_qkv = lax.ppermute(w_qkv, "batch", [(0, 1), (1, 0)])
    in_far = fetch(inputs)
    other_out = lax.ppermute(w_out, "batch", [(0, 1), (1, 0)])
    all_qkv = whole(w_qkv, other_qkv)
    all_out = whole(w_out, other_out)

    def project(x):
        normed, inverse = normalise(x)
        scaled = (normed * gain).astype(jnp.bfloat16)
        return nn(scaled, all_qkv).astype(jnp.bfloat16)

    in_core, cot_core = core(inputs), core(cotangent)
    qkv_core = project(in_core)
    up_core = nt(cot_core, all_out).astype(jnp.bfloat16)
    in_far = after(in_far, qkv_core, up_core)
    cot_far = fetch(after(cotangent, in_far))
    in_edge = jnp.where(foreign, in_far, edge(inputs))
    qkv_edge = project(in_edge)
    qkv = jnp.concatenate([qkv_edge, qkv_core], axis=0)
    attended, stats = attend(qkv)
    up_edge_rows = nn(attended[:half], all_out).astype(jnp.bfloat16)
    update_back = give_back(up_edge_rows)
    update_core = nn(attended[half:], all_out).astype(jnp.bfloat16)

    cot_far = after(cot_far, up_edge_rows)
    cot_edge = jnp.where(foreign, cot_far, edge(cotangent))
    up = jnp.concatenate([nt(cot_edge, all_out).astype(jnp.bfloat16), up_core], axis=0)
    grads = reverse(qkv, up, stats)

    def backward(rows, x):
        total = 0.0
        for index, piece in enumerate(grads):
            total = total + nt(piece[rows], all_qkv[:, index * channels : (index + 1) * channels])
        grad_normed = total * gain
        normed, inverse = normalise(x)
        mean_grad = jnp.mean(grad_normed, axis=-1, keepdims=True)
        mean_mixed = jnp.mean(grad_normed * normed, axis=-1, keepdims=True)
        return (inverse * (grad_normed - mean_grad - normed * mean_mixed)).astype(jnp.bfloat16)

    grad_edge = backward(slice(0, half), in_edge)
    grad_back = give_back(grad_edge)
    grad_core = backward(slice(half, tokens), in_core)
    update = place(up_edge_rows, update_back, update_core)
    grad = place(grad_edge, grad_back, grad_core)
    return update, grad


def solution(mesh):
    tiles = P(("groups", "batch"), "space", None, None, None, None)
    in_specs = (tiles, tiles, P(("groups", "batch")), P("batch", None), P("batch", None), P())
    return jax.shard_map(shards, mesh=mesh, in_specs=in_specs, out_specs=(tiles, tiles), check_vma=False)
```

```python
import functools

import jax
import jax.numpy as jnp
from jax import lax
from jax.experimental import pallas as pl
from jax.experimental.pallas import tpu as pltpu
from jax.sharding import PartitionSpec as P

YTILES = 4
HEAD_DIM = 64
EPS = 1e-05
PAIR = 2 * HEAD_DIM
SCALE = HEAD_DIM ** (-0.5)


def passed_along(x, by):
    size = lax.axis_size("space")
    return lax.ppermute(x, "space", [(i, (i + by) % size) for i in range(size)])


def nt(a, b):
    return lax.dot_general(a, b, (((1,), (1,)), ((), ())), preferred_element_type=jnp.float32)


def nn(a, b):
    return lax.dot_general(a, b, (((1,), (0,)), ((), ())), preferred_element_type=jnp.float32)


def only_head(x, head):
    lane = lax.broadcasted_iota(jnp.int32, x.shape, 1)
    keep = lane < HEAD_DIM if head == 0 else lane >= HEAD_DIM
    return jnp.where(keep, x, jnp.zeros_like(x))


def by_head(first, second):
    lane = lax.broadcasted_iota(jnp.int32, first.shape, 1)
    return jnp.where(lane < HEAD_DIM, first, second)


def attend_kernel(q_ref, k_ref, v_ref, o_ref, stats_ref):
    q, k = q_ref[...] * SCALE, k_ref[...]
    v_t = v_ref[...].T
    outs = []
    for head in range(2):
        scores = nt(k, only_head(q, head))
        peak = jnp.max(scores, axis=0, keepdims=True)
        raised = jnp.exp(scores - peak)
        inv = 1.0 / jnp.sum(raised, axis=0, keepdims=True)
        stats_ref[0, 2 * head : 2 * head + 1, :] = peak
        stats_ref[0, 2 * head + 1 : 2 * head + 2, :] = inv
        probs = (raised * inv).astype(jnp.bfloat16)
        outs.append(nn(v_t[HEAD_DIM * head : HEAD_DIM * (head + 1)], probs))
    o_ref[...] = jnp.concatenate(outs, axis=0).T.astype(jnp.bfloat16)


def reverse_kernel(q_ref, k_ref, v_ref, up_ref, stats_ref, dq_ref, dk_ref, dv_ref):
    q, k, v, up = q_ref[...] * SCALE, k_ref[...], v_ref[...], up_ref[...]
    k_t = (k * SCALE).T
    dqs, dks, dvs = [], [], []
    for head in range(2):
        scores = nt(k, only_head(q, head))
        peak = stats_ref[0, 2 * head : 2 * head + 1, :]
        inv = stats_ref[0, 2 * head + 1 : 2 * head + 2, :]
        probs = jnp.exp(scores - peak) * inv
        grad_probs = nt(v, only_head(up, head))
        delta = jnp.sum(grad_probs * probs, axis=0, keepdims=True)
        grad_scores = (probs * (grad_probs - delta)).astype(jnp.bfloat16)
        dqs.append(nn(k_t[HEAD_DIM * head : HEAD_DIM * (head + 1)], grad_scores))
        dks.append(nn(grad_scores, q))
        dvs.append(nn(probs.astype(jnp.bfloat16), up))
    dq_ref[...] = jnp.concatenate(dqs, axis=0).T.astype(jnp.bfloat16)
    dk_ref[...] = by_head(*dks).astype(jnp.bfloat16)
    dv_ref[...] = by_head(*dvs).astype(jnp.bfloat16)


def attend(qkv):
    tokens, width = qkv.shape
    channels = width // 3
    pairs = channels // PAIR

    def cols(which):
        return pl.BlockSpec((tokens, PAIR), lambda i: (0, which * pairs + i))

    return pl.pallas_call(
        attend_kernel,
        grid=(pairs,),
        in_specs=[cols(0), cols(1), cols(2)],
        out_specs=[cols(0), pl.BlockSpec((1, 4, tokens), lambda i: (i, 0, 0))],
        out_shape=[
            jax.ShapeDtypeStruct((tokens, channels), jnp.bfloat16),
            jax.ShapeDtypeStruct((pairs, 4, tokens), jnp.float32),
        ],
        compiler_params=pltpu.CompilerParams(vmem_limit_bytes=40 << 20),
        cost_estimate=pl.CostEstimate(
            flops=8 * tokens * tokens * channels,
            transcendentals=tokens * tokens * channels // HEAD_DIM,
            bytes_accessed=8 * tokens * channels,
        ),
        name="attend",
    )(qkv, qkv, qkv)


def reverse(qkv, up, stats):
    tokens, width = qkv.shape
    channels = width // 3
    pairs = channels // PAIR

    def cols(which):
        return pl.BlockSpec((tokens, PAIR), lambda i: (0, which * pairs + i))

    return pl.pallas_call(
        reverse_kernel,
        grid=(pairs,),
        in_specs=[cols(0), cols(1), cols(2), cols(0), pl.BlockSpec((1, 4, tokens), lambda i: (i, 0, 0))],
        out_specs=[cols(0), cols(0), cols(0)],
        out_shape=[jax.ShapeDtypeStruct((tokens, channels), jnp.bfloat16)] * 3,
        compiler_params=pltpu.CompilerParams(vmem_limit_bytes=40 << 20),
        cost_estimate=pl.CostEstimate(
            flops=20 * tokens * tokens * channels,
            transcendentals=tokens * tokens * channels // HEAD_DIM,
            bytes_accessed=14 * tokens * channels,
        ),
        name="reverse",
    )(qkv, qkv, qkv, up, stats)


def normalise(x):
    values32 = x.astype(jnp.float32)
    center = values32 - jnp.mean(values32, axis=-1, keepdims=True)
    inverse = lax.rsqrt(jnp.mean(center * center, axis=-1, keepdims=True) + EPS)
    return center * inverse, inverse


def shards(inputs, cotangent, offsets, w_qkv, w_out, gain):
    tiled_shape = inputs.shape
    slab, channels = tiled_shape[2], tiled_shape[-1]
    inputs = inputs.reshape(-1, channels)
    cotangent = cotangent.reshape(-1, channels)
    tokens = inputs.shape[0]
    half, plane = tokens // 2, tokens // slab
    start = offsets[0]
    upper = start > slab // 2
    two = lax.axis_size("space") == 2 * YTILES
    plane_of = lax.broadcasted_iota(jnp.int32, (half, 1), 0) // plane
    foreign = jnp.where(upper, plane_of + slab // 2 >= start, plane_of < start)

    def after(x, *earlier):
        return lax.optimization_barrier((x,) + earlier)[0]

    def edge(x):
        return lax.dynamic_slice_in_dim(x, jnp.where(upper, half, 0), half, 0)

    def core(x):
        return lax.dynamic_slice_in_dim(x, jnp.where(upper, 0, half), half, 0)

    def fetch(low, high):
        if two:
            return passed_along(jnp.where(upper, high, low), YTILES)
        return jnp.where(upper, passed_along(high, YTILES), passed_along(low, -YTILES))

    def give_back(x):
        if two:
            return passed_along(x, YTILES)
        return jnp.where(upper, passed_along(x, -YTILES), passed_along(x, YTILES))

    first = lax.axis_index("batch") == 0

    def whole(own, other):
        return jnp.concatenate([jnp.where(first, own, other), jnp.where(first, other, own)], axis=0)

    other_qkv = lax.ppermute(w_qkv, "batch", [(0, 1), (1, 0)])
    in_far = fetch(inputs[:half], inputs[half:])
    other_out = lax.ppermute(w_out, "batch", [(0, 1), (1, 0)])
    all_qkv = whole(w_qkv, other_qkv)
    all_out = whole(w_out, other_out)

    def project(x):
        normed, inverse = normalise(x)
        scaled = (normed * gain).astype(jnp.bfloat16)
        return nn(scaled, all_qkv).astype(jnp.bfloat16)

    in_core, cot_core = core(inputs), core(cotangent)
    qkv_core = project(in_core)
    up_core = nt(cot_core, all_out).astype(jnp.bfloat16)
    in_far = after(in_far, qkv_core, up_core)
    in_edge = jnp.where(foreign, in_far, edge(inputs))

    def rest(planes, operands):
        cotangent, in_edge, in_core, qkv_core, up_core, all_qkv, all_out = operands
        moved = planes * plane
        offset = jnp.where(upper, half - moved, 0)

        def put(x, rows):
            return lax.dynamic_update_slice_in_dim(x, rows, offset, 0)

        def take(x):
            return lax.dynamic_slice_in_dim(x, offset, moved, 0)

        cot_far = fetch(cotangent[:moved], cotangent[tokens - moved :])
        qkv = jnp.concatenate([project(in_edge), qkv_core], axis=0)
        attended, stats = attend(qkv)
        update_edge = nn(attended[:half], all_out).astype(jnp.bfloat16)
        cot_far = after(cot_far, update_edge)
        update_back = give_back(after(take(update_edge), cot_far))
        update_core = nn(attended[half:], all_out).astype(jnp.bfloat16)
        cot_edge = put(edge(cotangent), cot_far)
        up = jnp.concatenate([nt(cot_edge, all_out).astype(jnp.bfloat16), up_core], axis=0)
        grads = reverse(qkv, up, stats)

        def backward(rows, x):
            total = 0.0
            for index, piece in enumerate(grads):
                total = total + nt(piece[rows], all_qkv[:, index * channels : (index + 1) * channels])
            grad_normed = total * gain
            normed, inverse = normalise(x)
            mean_grad = jnp.mean(grad_normed, axis=-1, keepdims=True)
            mean_mixed = jnp.mean(grad_normed * normed, axis=-1, keepdims=True)
            return (inverse * (grad_normed - mean_grad - normed * mean_mixed)).astype(jnp.bfloat16)

        def place(edge_rows, back, core_rows):
            edge_rows = put(edge_rows, back)
            low = jnp.where(upper, core_rows, edge_rows)
            high = jnp.where(upper, edge_rows, core_rows)
            return jnp.concatenate([low, high], axis=0)

        grad_edge = backward(slice(0, half), in_edge)
        grad_back = give_back(take(grad_edge))
        grad_core = backward(slice(half, tokens), in_core)
        update = place(update_edge, update_back, update_core)
        grad = place(grad_edge, grad_back, grad_core)
        return update, grad

    travelling = jnp.where(upper, slab - start, start)
    update, grad = lax.switch(
        travelling - 1,
        [functools.partial(rest, planes) for planes in range(1, slab // 2 + 1)],
        (cotangent, in_edge, in_core, qkv_core, up_core, all_qkv, all_out),
    )
    return update.reshape(tiled_shape), grad.reshape(tiled_shape)


def solution(mesh):
    tiles = P(("groups", "batch"), "space", None, None, None, None)
    in_specs = (tiles, tiles, P(("groups", "batch")), P("batch", None), P("batch", None), P())
    return jax.shard_map(shards, mesh=mesh, in_specs=in_specs, out_specs=(tiles, tiles), check_vma=False)
```

```python
import jax
import jax.numpy as jnp
from jax import lax
from jax.experimental import pallas as pl
from jax.experimental.pallas import tpu as pltpu
from jax.sharding import PartitionSpec as P

YTILES = 4
HEAD_DIM = 64
EPS = 1e-05
PAIR = 2 * HEAD_DIM
SCALE = HEAD_DIM ** (-0.5)


def passed_along(x, by):
    size = lax.axis_size("space")
    return lax.ppermute(x, "space", [(i, (i + by) % size) for i in range(size)])


def nt(a, b):
    return lax.dot_general(a, b, (((1,), (1,)), ((), ())), preferred_element_type=jnp.float32)


def nn(a, b):
    return lax.dot_general(a, b, (((1,), (0,)), ((), ())), preferred_element_type=jnp.float32)


def only_head(x, head):
    lane = lax.broadcasted_iota(jnp.int32, x.shape, 1)
    keep = lane < HEAD_DIM if head == 0 else lane >= HEAD_DIM
    return jnp.where(keep, x, jnp.zeros_like(x))


def by_head(first, second):
    lane = lax.broadcasted_iota(jnp.int32, first.shape, 1)
    return jnp.where(lane < HEAD_DIM, first, second)


def attend_kernel(q_ref, k_ref, v_ref, o_ref, stats_ref):
    q, k = q_ref[...] * SCALE, k_ref[...]
    v_t = v_ref[...].T
    outs = []
    for head in range(2):
        scores = nt(k, only_head(q, head))
        peak = jnp.max(scores, axis=0, keepdims=True)
        raised = jnp.exp(scores - peak)
        inv = 1.0 / jnp.sum(raised, axis=0, keepdims=True)
        stats_ref[0, 2 * head : 2 * head + 1, :] = peak
        stats_ref[0, 2 * head + 1 : 2 * head + 2, :] = inv
        probs = (raised * inv).astype(jnp.bfloat16)
        outs.append(nn(v_t[HEAD_DIM * head : HEAD_DIM * (head + 1)], probs))
    o_ref[...] = jnp.concatenate(outs, axis=0).T.astype(jnp.bfloat16)


def reverse_kernel(q_ref, k_ref, v_ref, up_ref, stats_ref, dq_ref, dk_ref, dv_ref):
    q, k, v, up = q_ref[...] * SCALE, k_ref[...], v_ref[...], up_ref[...]
    k_t = (k * SCALE).T
    dqs, dks, dvs = [], [], []
    for head in range(2):
        scores = nt(k, only_head(q, head))
        peak = stats_ref[0, 2 * head : 2 * head + 1, :]
        inv = stats_ref[0, 2 * head + 1 : 2 * head + 2, :]
        probs = jnp.exp(scores - peak) * inv
        grad_probs = nt(v, only_head(up, head))
        delta = jnp.sum(grad_probs * probs, axis=0, keepdims=True)
        grad_scores = (probs * (grad_probs - delta)).astype(jnp.bfloat16)
        dqs.append(nn(k_t[HEAD_DIM * head : HEAD_DIM * (head + 1)], grad_scores))
        dks.append(nn(grad_scores, q))
        dvs.append(nn(probs.astype(jnp.bfloat16), up))
    dq_ref[...] = jnp.concatenate(dqs, axis=0).T.astype(jnp.bfloat16)
    dk_ref[...] = by_head(*dks).astype(jnp.bfloat16)
    dv_ref[...] = by_head(*dvs).astype(jnp.bfloat16)


def attend(qkv):
    tokens, width = qkv.shape
    channels = width // 3
    pairs = channels // PAIR

    def cols(which):
        return pl.BlockSpec((tokens, PAIR), lambda i: (0, which * pairs + i))

    return pl.pallas_call(
        attend_kernel,
        grid=(pairs,),
        in_specs=[cols(0), cols(1), cols(2)],
        out_specs=[cols(0), pl.BlockSpec((1, 4, tokens), lambda i: (i, 0, 0))],
        out_shape=[
            jax.ShapeDtypeStruct((tokens, channels), jnp.bfloat16),
            jax.ShapeDtypeStruct((pairs, 4, tokens), jnp.float32),
        ],
        compiler_params=pltpu.CompilerParams(vmem_limit_bytes=40 << 20),
        cost_estimate=pl.CostEstimate(
            flops=8 * tokens * tokens * channels,
            transcendentals=tokens * tokens * channels // HEAD_DIM,
            bytes_accessed=8 * tokens * channels,
        ),
        name="attend",
    )(qkv, qkv, qkv)


def reverse(qkv, up, stats):
    tokens, width = qkv.shape
    channels = width // 3
    pairs = channels // PAIR

    def cols(which):
        return pl.BlockSpec((tokens, PAIR), lambda i: (0, which * pairs + i))

    return pl.pallas_call(
        reverse_kernel,
        grid=(pairs,),
        in_specs=[cols(0), cols(1), cols(2), cols(0), pl.BlockSpec((1, 4, tokens), lambda i: (i, 0, 0))],
        out_specs=[cols(0), cols(0), cols(0)],
        out_shape=[jax.ShapeDtypeStruct((tokens, channels), jnp.bfloat16)] * 3,
        compiler_params=pltpu.CompilerParams(vmem_limit_bytes=40 << 20),
        cost_estimate=pl.CostEstimate(
            flops=20 * tokens * tokens * channels,
            transcendentals=tokens * tokens * channels // HEAD_DIM,
            bytes_accessed=14 * tokens * channels,
        ),
        name="reverse",
    )(qkv, qkv, qkv, up, stats)


def normalise(x):
    values32 = x.astype(jnp.float32)
    center = values32 - jnp.mean(values32, axis=-1, keepdims=True)
    inverse = lax.rsqrt(jnp.mean(center * center, axis=-1, keepdims=True) + EPS)
    return center * inverse, inverse


def shards(inputs, cotangent, offsets, w_qkv, w_out, gain):
    tiled_shape = inputs.shape
    slab, channels = tiled_shape[2], tiled_shape[-1]
    inputs = inputs.reshape(-1, channels)
    cotangent = cotangent.reshape(-1, channels)
    tokens = inputs.shape[0]
    half, plane = tokens // 2, tokens // slab
    start = offsets[0]
    upper = start > slab // 2
    two = lax.axis_size("space") == 2 * YTILES
    plane_of = lax.broadcasted_iota(jnp.int32, (half, 1), 0) // plane
    foreign = jnp.where(upper, plane_of + slab // 2 >= start, plane_of < start)

    def edge(x):
        return lax.dynamic_slice_in_dim(x, jnp.where(upper, half, 0), half, 0)

    def core(x):
        return lax.dynamic_slice_in_dim(x, jnp.where(upper, 0, half), half, 0)

    def after(x, *earlier):
        return lax.optimization_barrier((x,) + earlier)[0]

    def fetch(x):
        if two:
            return passed_along(edge(x), YTILES)
        return jnp.where(upper, passed_along(x[half:], YTILES), passed_along(x[:half], -YTILES))

    def give_back(x):
        if two:
            return passed_along(x, YTILES)
        return jnp.where(upper, passed_along(x, -YTILES), passed_along(x, YTILES))

    def place(edge_mine, edge_back, core_mine):
        edge_out = jnp.where(foreign, edge_back, edge_mine)
        low = jnp.where(upper, core_mine, edge_out)
        high = jnp.where(upper, edge_out, core_mine)
        return jnp.concatenate([low, high], axis=0).reshape(tiled_shape)

    first = lax.axis_index("batch") == 0

    def whole(own, other):
        return jnp.concatenate([jnp.where(first, own, other), jnp.where(first, other, own)], axis=0)

    other_qkv = lax.ppermute(w_qkv, "batch", [(0, 1), (1, 0)])
    in_far = fetch(inputs)
    other_out = lax.ppermute(w_out, "batch", [(0, 1), (1, 0)])
    all_qkv = whole(w_qkv, other_qkv)
    all_out = whole(w_out, other_out)

    def project(x):
        normed, inverse = normalise(x)
        scaled = (normed * gain).astype(jnp.bfloat16)
        return nn(scaled, all_qkv).astype(jnp.bfloat16)

    in_core, cot_core = core(inputs), core(cotangent)
    qkv_core = project(in_core)
    up_core = nt(cot_core, all_out).astype(jnp.bfloat16)
    in_far = after(in_far, qkv_core, up_core)
    cot_far = fetch(after(cotangent, in_far))
    in_edge = jnp.where(foreign, in_far, edge(inputs))
    qkv_edge = project(in_edge)
    qkv = jnp.concatenate([qkv_edge, qkv_core], axis=0)
    attended, stats = attend(qkv)
    up_edge_rows = nn(attended[:half], all_out).astype(jnp.bfloat16)
    update_core = nn(attended[half:], all_out).astype(jnp.bfloat16)

    cot_far = after(cot_far, up_edge_rows)
    update_back = give_back(after(up_edge_rows, cot_far))
    cot_edge = jnp.where(foreign, cot_far, edge(cotangent))
    up = jnp.concatenate([nt(cot_edge, all_out).astype(jnp.bfloat16), up_core], axis=0)
    *grads, update_back = lax.optimization_barrier((*reverse(qkv, up, stats), update_back))

    def backward(rows, x):
        total = 0.0
        for index, piece in enumerate(grads):
            total = total + nt(piece[rows], all_qkv[:, index * channels : (index + 1) * channels])
        grad_normed = total * gain
        normed, inverse = normalise(x)
        mean_grad = jnp.mean(grad_normed, axis=-1, keepdims=True)
        mean_mixed = jnp.mean(grad_normed * normed, axis=-1, keepdims=True)
        return (inverse * (grad_normed - mean_grad - normed * mean_mixed)).astype(jnp.bfloat16)

    grad_edge = backward(slice(0, half), in_edge)
    grad_back = give_back(grad_edge)
    grad_core = backward(slice(half, tokens), in_core)
    update = place(up_edge_rows, update_back, update_core)
    grad = place(grad_edge, grad_back, grad_core)
    return update, grad


def solution(mesh):
    tiles = P(("groups", "batch"), "space", None, None, None, None)
    in_specs = (tiles, tiles, P(("groups", "batch")), P("batch", None), P("batch", None), P())
    return jax.shard_map(shards, mesh=mesh, in_specs=in_specs, out_specs=(tiles, tiles), check_vma=False)
```

```python
import functools

import jax
import jax.numpy as jnp
from jax import lax
from jax.experimental import pallas as pl
from jax.experimental.pallas import tpu as pltpu
from jax.sharding import PartitionSpec as P

YTILES = 4
HEAD_DIM = 64
EPS = 1e-05
PAIR = 2 * HEAD_DIM
SCALE = HEAD_DIM ** (-0.5)


def passed_along(x, by):
    size = lax.axis_size("space")
    return lax.ppermute(x, "space", [(i, (i + by) % size) for i in range(size)])


def nt(a, b):
    return lax.dot_general(a, b, (((1,), (1,)), ((), ())), preferred_element_type=jnp.float32)


def nn(a, b):
    return lax.dot_general(a, b, (((1,), (0,)), ((), ())), preferred_element_type=jnp.float32)


def only_head(x, head):
    lane = lax.broadcasted_iota(jnp.int32, x.shape, 1)
    keep = lane < HEAD_DIM if head == 0 else lane >= HEAD_DIM
    return jnp.where(keep, x, jnp.zeros_like(x))


def by_head(first, second):
    lane = lax.broadcasted_iota(jnp.int32, first.shape, 1)
    return jnp.where(lane < HEAD_DIM, first, second)


def attend_kernel(q_ref, k_ref, v_ref, o_ref, stats_ref):
    q, k = q_ref[...] * SCALE, k_ref[...]
    v_t = v_ref[...].T
    outs = []
    for head in range(2):
        scores = nt(k, only_head(q, head))
        peak = jnp.max(scores, axis=0, keepdims=True)
        raised = jnp.exp(scores - peak)
        inv = 1.0 / jnp.sum(raised, axis=0, keepdims=True)
        stats_ref[0, 2 * head : 2 * head + 1, :] = peak
        stats_ref[0, 2 * head + 1 : 2 * head + 2, :] = inv
        probs = (raised * inv).astype(jnp.bfloat16)
        outs.append(nn(v_t[HEAD_DIM * head : HEAD_DIM * (head + 1)], probs))
    o_ref[...] = jnp.concatenate(outs, axis=0).T.astype(jnp.bfloat16)


def reverse_kernel(q_ref, k_ref, v_ref, up_ref, stats_ref, dq_ref, dk_ref, dv_ref):
    q, k, v, up = q_ref[...] * SCALE, k_ref[...], v_ref[...], up_ref[...]
    k_t = (k * SCALE).T
    dqs, dks, dvs = [], [], []
    for head in range(2):
        scores = nt(k, only_head(q, head))
        peak = stats_ref[0, 2 * head : 2 * head + 1, :]
        inv = stats_ref[0, 2 * head + 1 : 2 * head + 2, :]
        probs = jnp.exp(scores - peak) * inv
        grad_probs = nt(v, only_head(up, head))
        delta = jnp.sum(grad_probs * probs, axis=0, keepdims=True)
        grad_scores = (probs * (grad_probs - delta)).astype(jnp.bfloat16)
        dqs.append(nn(k_t[HEAD_DIM * head : HEAD_DIM * (head + 1)], grad_scores))
        dks.append(nn(grad_scores, q))
        dvs.append(nn(probs.astype(jnp.bfloat16), up))
    dq_ref[...] = jnp.concatenate(dqs, axis=0).T.astype(jnp.bfloat16)
    dk_ref[...] = by_head(*dks).astype(jnp.bfloat16)
    dv_ref[...] = by_head(*dvs).astype(jnp.bfloat16)


def attend(qkv):
    tokens, width = qkv.shape
    channels = width // 3
    pairs = channels // PAIR

    def cols(which):
        return pl.BlockSpec((tokens, PAIR), lambda i: (0, which * pairs + i))

    return pl.pallas_call(
        attend_kernel,
        grid=(pairs,),
        in_specs=[cols(0), cols(1), cols(2)],
        out_specs=[cols(0), pl.BlockSpec((1, 4, tokens), lambda i: (i, 0, 0))],
        out_shape=[
            jax.ShapeDtypeStruct((tokens, channels), jnp.bfloat16),
            jax.ShapeDtypeStruct((pairs, 4, tokens), jnp.float32),
        ],
        compiler_params=pltpu.CompilerParams(vmem_limit_bytes=40 << 20),
        cost_estimate=pl.CostEstimate(
            flops=8 * tokens * tokens * channels,
            transcendentals=tokens * tokens * channels // HEAD_DIM,
            bytes_accessed=8 * tokens * channels,
        ),
        name="attend",
    )(qkv, qkv, qkv)


def reverse(qkv, up, stats):
    tokens, width = qkv.shape
    channels = width // 3
    pairs = channels // PAIR

    def cols(which):
        return pl.BlockSpec((tokens, PAIR), lambda i: (0, which * pairs + i))

    return pl.pallas_call(
        reverse_kernel,
        grid=(pairs,),
        in_specs=[cols(0), cols(1), cols(2), cols(0), pl.BlockSpec((1, 4, tokens), lambda i: (i, 0, 0))],
        out_specs=[cols(0), cols(0), cols(0)],
        out_shape=[jax.ShapeDtypeStruct((tokens, channels), jnp.bfloat16)] * 3,
        compiler_params=pltpu.CompilerParams(vmem_limit_bytes=40 << 20),
        cost_estimate=pl.CostEstimate(
            flops=20 * tokens * tokens * channels,
            transcendentals=tokens * tokens * channels // HEAD_DIM,
            bytes_accessed=14 * tokens * channels,
        ),
        name="reverse",
    )(qkv, qkv, qkv, up, stats)


def normalise(x):
    values32 = x.astype(jnp.float32)
    center = values32 - jnp.mean(values32, axis=-1, keepdims=True)
    inverse = lax.rsqrt(jnp.mean(center * center, axis=-1, keepdims=True) + EPS)
    return center * inverse, inverse


def shards(inputs, cotangent, offsets, w_qkv, w_out, gain):
    tiled_shape = inputs.shape
    slab, channels = tiled_shape[2], tiled_shape[-1]
    inputs = inputs.reshape(-1, channels)
    cotangent = cotangent.reshape(-1, channels)
    tokens = inputs.shape[0]
    half, plane = tokens // 2, tokens // slab
    start = offsets[0]
    upper = start > slab // 2
    two = lax.axis_size("space") == 2 * YTILES
    plane_of = lax.broadcasted_iota(jnp.int32, (half, 1), 0) // plane
    foreign = jnp.where(upper, plane_of + slab // 2 >= start, plane_of < start)

    def edge(x):
        return lax.dynamic_slice_in_dim(x, jnp.where(upper, half, 0), half, 0)

    def core(x):
        return lax.dynamic_slice_in_dim(x, jnp.where(upper, 0, half), half, 0)

    def after(x, *earlier):
        return lax.optimization_barrier((x,) + earlier)[0]

    def fetch(x):
        if two:
            return passed_along(edge(x), YTILES)
        return jnp.where(upper, passed_along(x[half:], YTILES), passed_along(x[:half], -YTILES))

    def give_back(x):
        if two:
            return passed_along(x, YTILES)
        return jnp.where(upper, passed_along(x, -YTILES), passed_along(x, YTILES))

    def place(edge_mine, edge_back, core_mine):
        edge_out = jnp.where(foreign, edge_back, edge_mine)
        low = jnp.where(upper, core_mine, edge_out)
        high = jnp.where(upper, edge_out, core_mine)
        return jnp.concatenate([low, high], axis=0).reshape(tiled_shape)

    first = lax.axis_index("batch") == 0

    def whole(own, other):
        return jnp.concatenate([jnp.where(first, own, other), jnp.where(first, other, own)], axis=0)

    other_qkv = lax.ppermute(w_qkv, "batch", [(0, 1), (1, 0)])
    in_far = fetch(inputs)
    other_out = lax.ppermute(w_out, "batch", [(0, 1), (1, 0)])
    all_qkv = whole(w_qkv, other_qkv)
    all_out = whole(w_out, other_out)

    def project(x):
        normed, inverse = normalise(x)
        scaled = (normed * gain).astype(jnp.bfloat16)
        return nn(scaled, all_qkv).astype(jnp.bfloat16)

    in_core, cot_core = core(inputs), core(cotangent)
    qkv_core = project(in_core)
    up_core = nt(cot_core, all_out).astype(jnp.bfloat16)
    in_far = after(in_far, qkv_core, up_core)
    cot_far = fetch(after(cotangent, in_far))
    in_edge = jnp.where(foreign, in_far, edge(inputs))
    qkv_edge = project(in_edge)
    qkv = jnp.concatenate([qkv_edge, qkv_core], axis=0)
    attended, stats = attend(qkv)
    up_edge_rows = nn(attended[:half], all_out).astype(jnp.bfloat16)
    update_core = nn(attended[half:], all_out).astype(jnp.bfloat16)

    cot_far = after(cot_far, up_edge_rows)
    update_back = give_back(after(up_edge_rows, cot_far))
    cot_edge = jnp.where(foreign, cot_far, edge(cotangent))
    up = jnp.concatenate([nt(cot_edge, all_out).astype(jnp.bfloat16), up_core], axis=0)
    *grads, update_back = lax.optimization_barrier((*reverse(qkv, up, stats), update_back))

    def backward(rows, x, grads):
        total = 0.0
        for index, piece in enumerate(grads):
            total = total + nt(piece[rows], all_qkv[:, index * channels : (index + 1) * channels])
        grad_normed = total * gain
        normed, inverse = normalise(x)
        mean_grad = jnp.mean(grad_normed, axis=-1, keepdims=True)
        mean_mixed = jnp.mean(grad_normed * normed, axis=-1, keepdims=True)
        return (inverse * (grad_normed - mean_grad - normed * mean_mixed)).astype(jnp.bfloat16)

    grad_edge = backward(slice(0, half), in_edge, grads)
    update_back, grad_edge = lax.optimization_barrier((update_back, grad_edge))

    def last(planes, operands):
        grad_edge, up_edge_rows, update_back, update_core, in_core, *pieces = operands
        moved = planes * plane
        offset = jnp.where(upper, half - moved, 0)
        back = give_back(lax.dynamic_slice_in_dim(grad_edge, offset, moved, 0))
        grad_core = backward(slice(half, tokens), in_core, pieces)
        update = place(up_edge_rows, update_back, update_core)
        back = after(back, grad_core, update)
        edge_rows = lax.dynamic_update_slice_in_dim(grad_edge, back, offset, 0)
        low = jnp.where(upper, grad_core, edge_rows)
        high = jnp.where(upper, edge_rows, grad_core)
        return update, jnp.concatenate([low, high], axis=0).reshape(tiled_shape)

    travelling = jnp.where(upper, slab - start, start)
    return lax.switch(
        travelling - 1,
        [functools.partial(last, planes) for planes in range(1, slab // 2 + 1)],
        (grad_edge, up_edge_rows, update_back, update_core, in_core, *grads),
    )


def solution(mesh):
    tiles = P(("groups", "batch"), "space", None, None, None, None)
    in_specs = (tiles, tiles, P(("groups", "batch")), P("batch", None), P("batch", None), P())
    return jax.shard_map(shards, mesh=mesh, in_specs=in_specs, out_specs=(tiles, tiles), check_vma=False)
```

```python
import functools

import jax
import jax.numpy as jnp
from jax import lax
from jax.experimental import pallas as pl
from jax.experimental.pallas import tpu as pltpu
from jax.sharding import PartitionSpec as P

YTILES = 4
HEAD_DIM = 64
EPS = 1e-05
PAIR = 2 * HEAD_DIM
SCALE = HEAD_DIM ** (-0.5)


def passed_along(x, by):
    size = lax.axis_size("space")
    return lax.ppermute(x, "space", [(i, (i + by) % size) for i in range(size)])


def nt(a, b):
    return lax.dot_general(a, b, (((1,), (1,)), ((), ())), preferred_element_type=jnp.float32)


def nn(a, b):
    return lax.dot_general(a, b, (((1,), (0,)), ((), ())), preferred_element_type=jnp.float32)


def only_head(x, head):
    lane = lax.broadcasted_iota(jnp.int32, x.shape, 1)
    keep = lane < HEAD_DIM if head == 0 else lane >= HEAD_DIM
    return jnp.where(keep, x, jnp.zeros_like(x))


def by_head(first, second):
    lane = lax.broadcasted_iota(jnp.int32, first.shape, 1)
    return jnp.where(lane < HEAD_DIM, first, second)


def attend_kernel(q_ref, k_ref, v_ref, o_ref, stats_ref):
    q, k = q_ref[...] * SCALE, k_ref[...]
    v_t = v_ref[...].T
    outs = []
    for head in range(2):
        scores = nt(k, only_head(q, head))
        peak = jnp.max(scores, axis=0, keepdims=True)
        raised = jnp.exp(scores - peak)
        inv = 1.0 / jnp.sum(raised, axis=0, keepdims=True)
        stats_ref[0, 2 * head : 2 * head + 1, :] = peak
        stats_ref[0, 2 * head + 1 : 2 * head + 2, :] = inv
        probs = (raised * inv).astype(jnp.bfloat16)
        outs.append(nn(v_t[HEAD_DIM * head : HEAD_DIM * (head + 1)], probs))
    o_ref[...] = jnp.concatenate(outs, axis=0).T.astype(jnp.bfloat16)


def reverse_kernel(q_ref, k_ref, v_ref, up_ref, stats_ref, dq_ref, dk_ref, dv_ref):
    q, k, v, up = q_ref[...] * SCALE, k_ref[...], v_ref[...], up_ref[...]
    k_t = (k * SCALE).T
    dqs, dks, dvs = [], [], []
    for head in range(2):
        scores = nt(k, only_head(q, head))
        peak = stats_ref[0, 2 * head : 2 * head + 1, :]
        inv = stats_ref[0, 2 * head + 1 : 2 * head + 2, :]
        probs = jnp.exp(scores - peak) * inv
        grad_probs = nt(v, only_head(up, head))
        delta = jnp.sum(grad_probs * probs, axis=0, keepdims=True)
        grad_scores = (probs * (grad_probs - delta)).astype(jnp.bfloat16)
        dqs.append(nn(k_t[HEAD_DIM * head : HEAD_DIM * (head + 1)], grad_scores))
        dks.append(nn(grad_scores, q))
        dvs.append(nn(probs.astype(jnp.bfloat16), up))
    dq_ref[...] = jnp.concatenate(dqs, axis=0).T.astype(jnp.bfloat16)
    dk_ref[...] = by_head(*dks).astype(jnp.bfloat16)
    dv_ref[...] = by_head(*dvs).astype(jnp.bfloat16)


def attend(qkv):
    tokens, width = qkv.shape
    channels = width // 3
    pairs = channels // PAIR

    def cols(which):
        return pl.BlockSpec((tokens, PAIR), lambda i: (0, which * pairs + i))

    return pl.pallas_call(
        attend_kernel,
        grid=(pairs,),
        in_specs=[cols(0), cols(1), cols(2)],
        out_specs=[cols(0), pl.BlockSpec((1, 4, tokens), lambda i: (i, 0, 0))],
        out_shape=[
            jax.ShapeDtypeStruct((tokens, channels), jnp.bfloat16),
            jax.ShapeDtypeStruct((pairs, 4, tokens), jnp.float32),
        ],
        compiler_params=pltpu.CompilerParams(vmem_limit_bytes=40 << 20),
        cost_estimate=pl.CostEstimate(
            flops=8 * tokens * tokens * channels,
            transcendentals=tokens * tokens * channels // HEAD_DIM,
            bytes_accessed=8 * tokens * channels,
        ),
        name="attend",
    )(qkv, qkv, qkv)


def reverse(qkv, up, stats):
    tokens, width = qkv.shape
    channels = width // 3
    pairs = channels // PAIR

    def cols(which):
        return pl.BlockSpec((tokens, PAIR), lambda i: (0, which * pairs + i))

    return pl.pallas_call(
        reverse_kernel,
        grid=(pairs,),
        in_specs=[cols(0), cols(1), cols(2), cols(0), pl.BlockSpec((1, 4, tokens), lambda i: (i, 0, 0))],
        out_specs=[cols(0), cols(0), cols(0)],
        out_shape=[jax.ShapeDtypeStruct((tokens, channels), jnp.bfloat16)] * 3,
        compiler_params=pltpu.CompilerParams(vmem_limit_bytes=40 << 20),
        cost_estimate=pl.CostEstimate(
            flops=20 * tokens * tokens * channels,
            transcendentals=tokens * tokens * channels // HEAD_DIM,
            bytes_accessed=14 * tokens * channels,
        ),
        name="reverse",
    )(qkv, qkv, qkv, up, stats)


def normalise(x):
    values32 = x.astype(jnp.float32)
    center = values32 - jnp.mean(values32, axis=-1, keepdims=True)
    inverse = lax.rsqrt(jnp.mean(center * center, axis=-1, keepdims=True) + EPS)
    return center * inverse, inverse


def shards(inputs, cotangent, offsets, w_qkv, w_out, gain):
    tiled_shape = inputs.shape
    slab, channels = tiled_shape[2], tiled_shape[-1]
    inputs = inputs.reshape(-1, channels)
    cotangent = cotangent.reshape(-1, channels)
    tokens = inputs.shape[0]
    half, plane = tokens // 2, tokens // slab
    start = offsets[0]
    upper = start > slab // 2
    two = lax.axis_size("space") == 2 * YTILES
    plane_of = lax.broadcasted_iota(jnp.int32, (half, 1), 0) // plane
    foreign = jnp.where(upper, plane_of + slab // 2 >= start, plane_of < start)

    def edge(x):
        return lax.dynamic_slice_in_dim(x, jnp.where(upper, half, 0), half, 0)

    def core(x):
        return lax.dynamic_slice_in_dim(x, jnp.where(upper, 0, half), half, 0)

    def after(x, *earlier):
        return lax.optimization_barrier((x,) + earlier)[0]

    def fetch(x):
        if two:
            return passed_along(edge(x), YTILES)
        return jnp.where(upper, passed_along(x[half:], YTILES), passed_along(x[:half], -YTILES))

    def give_back(x):
        if two:
            return passed_along(x, YTILES)
        return jnp.where(upper, passed_along(x, -YTILES), passed_along(x, YTILES))

    def place(edge_mine, edge_back, core_mine):
        edge_out = jnp.where(foreign, edge_back, edge_mine)
        low = jnp.where(upper, core_mine, edge_out)
        high = jnp.where(upper, edge_out, core_mine)
        return jnp.concatenate([low, high], axis=0).reshape(tiled_shape)

    first = lax.axis_index("batch") == 0

    def whole(own, other):
        return jnp.concatenate([jnp.where(first, own, other), jnp.where(first, other, own)], axis=0)

    other_qkv = lax.ppermute(w_qkv, "batch", [(0, 1), (1, 0)])
    in_far = fetch(inputs)
    other_out = lax.ppermute(w_out, "batch", [(0, 1), (1, 0)])
    all_qkv = whole(w_qkv, other_qkv)
    all_out = whole(w_out, other_out)

    def project(x):
        normed, inverse = normalise(x)
        scaled = (normed * gain).astype(jnp.bfloat16)
        return nn(scaled, all_qkv).astype(jnp.bfloat16)

    in_core, cot_core = core(inputs), core(cotangent)
    qkv_core = project(in_core)
    up_core = nt(cot_core, all_out).astype(jnp.bfloat16)
    in_far = after(in_far, qkv_core, up_core)
    cot_far = fetch(after(cotangent, in_far))
    in_edge = jnp.where(foreign, in_far, edge(inputs))
    qkv_edge = project(in_edge)
    qkv = jnp.concatenate([qkv_edge, qkv_core], axis=0)
    attended, stats = attend(qkv)
    attended, stats, cot_far = lax.optimization_barrier((attended, stats, cot_far))
    up_edge_rows = nn(attended[:half], all_out).astype(jnp.bfloat16)
    update_core = nn(attended[half:], all_out).astype(jnp.bfloat16)

    update_back = give_back(up_edge_rows)
    cot_edge = jnp.where(foreign, cot_far, edge(cotangent))
    up = jnp.concatenate([nt(cot_edge, all_out).astype(jnp.bfloat16), up_core], axis=0)
    *grads, update_back = lax.optimization_barrier((*reverse(qkv, up, stats), update_back))

    def backward(rows, x, grads):
        total = 0.0
        for index, piece in enumerate(grads):
            total = total + nt(piece[rows], all_qkv[:, index * channels : (index + 1) * channels])
        grad_normed = total * gain
        normed, inverse = normalise(x)
        mean_grad = jnp.mean(grad_normed, axis=-1, keepdims=True)
        mean_mixed = jnp.mean(grad_normed * normed, axis=-1, keepdims=True)
        return (inverse * (grad_normed - mean_grad - normed * mean_mixed)).astype(jnp.bfloat16)

    grad_edge = backward(slice(0, half), in_edge, grads)
    update_back, grad_edge = lax.optimization_barrier((update_back, grad_edge))

    def last(planes, operands):
        grad_edge, up_edge_rows, update_back, update_core, in_core, *pieces = operands
        moved = planes * plane
        offset = jnp.where(upper, half - moved, 0)
        back = give_back(lax.dynamic_slice_in_dim(grad_edge, offset, moved, 0))
        grad_core = backward(slice(half, tokens), in_core, pieces)
        update = place(up_edge_rows, update_back, update_core)
        back = after(back, grad_core, update)
        edge_rows = lax.dynamic_update_slice_in_dim(grad_edge, back, offset, 0)
        low = jnp.where(upper, grad_core, edge_rows)
        high = jnp.where(upper, edge_rows, grad_core)
        return update, jnp.concatenate([low, high], axis=0).reshape(tiled_shape)

    travelling = jnp.where(upper, slab - start, start)
    return lax.switch(
        travelling - 1,
        [functools.partial(last, planes) for planes in range(1, slab // 2 + 1)],
        (grad_edge, up_edge_rows, update_back, update_core, in_core, *grads),
    )


def solution(mesh):
    tiles = P(("groups", "batch"), "space", None, None, None, None)
    in_specs = (tiles, tiles, P(("groups", "batch")), P("batch", None), P("batch", None), P())
    return jax.shard_map(shards, mesh=mesh, in_specs=in_specs, out_specs=(tiles, tiles), check_vma=False)
```
